32 devices in a mesh: gx: 8 (over z, x), gy: 4 (over y, core).
Axes of the slice: x: 2, y: 2, z: 4, core: 2. Of those that a mesh axis runs over, the one named last changes fastest.
Arguments:
- reference_scan: bfloat16 [128, 128, 2048], P('gx', 'gy'), may hold values from -6 to 6
- ref_gradient: bfloat16 [3, 128, 128, 2048], P(None, 'gx', 'gy'), may hold values from -6 to 6
- deformed_scan: bfloat16 [128, 128, 2048], P('gx', 'gy'), may hold values from -6 to 6
- interp_weights: bfloat16 [128, 128, 2048], P('gx', 'gy'), may hold values from 0 to 1
- sample_mask: int32 [128, 128, 2048], P('gx', 'gy'), may hold values from 0 to 1, as said below
- block_list: int32 [8, 16384], P('gx', 'gy'), may hold values from -1 to 8191, as said below
- offsets: int32 [2, 128, 128, 4], P(None, 'gx', 'gy'), may hold values from -4 to 4, as said below
Outputs:
- increment: float32 [3, 128, 128, 5], P(None, 'gx', 'gy')
- cg_residual: float32 [3, 128, 128, 5], P(None, 'gx', 'gy')
The draws below stay inside these ranges and needn't reach their ends.
Inputs may be any that keep to these rules, and one draw needn't show every extreme that they name: sample_mask is 0 in every block of 128 voxels that its device's block_list does not name. `block_list`: each device's 4096 entries are first distinct local block indices, then -1 to the end; some device names exactly 4096 blocks. `offsets`: both ends of the range occur.
All inputs are finite; a program needn't handle non-finite values.
Results may differ from the reference program's by a relative error of at most 0.0045.
Values may be sent and summed in bfloat16 or wider, within the bound.
A program may use at most 320 MiB of HBM per device.

```python
import jax
import jax.numpy as jnp
from jax import lax

EX = 16
EY = 32
EZ = 4
BOUND = 4
ITERS = 3
CAP = 4096
NEX = 128
NEY = 128
N_GX = 8
N_GY = 4


def live_blocks(key):
    base = jax.random.fold_in(key, 4021)
    split_keys = jax.random.split(base, 4)
    devices_total = N_GX * N_GY
    local_blocks = EX * EY * EZ * 4
    counts = jax.random.randint(split_keys[0], (devices_total,), CAP // 8, CAP + 1)
    busiest = jax.random.randint(split_keys[1], (), 0, devices_total)
    counts = jnp.where(jnp.arange(devices_total) == busiest, CAP, counts)
    orders = jax.vmap(lambda inner: jax.random.permutation(inner, local_blocks))(jax.random.split(split_keys[2], devices_total))
    ranks = jnp.argsort(orders, axis=1)
    listed = (ranks < counts[:, None]).astype(jnp.int32)
    chosen = jnp.where(jnp.arange(CAP)[None, :] < counts[:, None], orders[:, :CAP], -1)
    voxels = (jax.random.randint(split_keys[3], (devices_total, local_blocks, 128), 0, 10) < 6).astype(jnp.int32)
    voxels = voxels * listed[:, :, None]
    return (chosen.astype(jnp.int32), voxels)


def draw_sample_mask(key, part):
    chosen, voxels = live_blocks(key)
    grid = jnp.transpose(voxels.reshape(N_GX, N_GY, EX, EY, EZ * 512), (0, 2, 1, 3, 4))
    return grid.reshape(EX * N_GX, EY * N_GY, EZ * 512).astype(jnp.int32)


def draw_block_list(key, part):
    chosen, voxels = live_blocks(key)
    return chosen.reshape(N_GX, N_GY * CAP).astype(jnp.int32)


def draw_offsets(key, part):
    inner = jax.random.fold_in(key, 733)
    values = jax.random.randint(inner, (2, EX * N_GX, EY * N_GY, EZ), -BOUND, BOUND + 1)
    values = values.at[:, 0, 0, 0].set(BOUND)
    values = values.at[:, EX * N_GX - 1, EY * N_GY - 1, EZ - 1].set(-BOUND)
    return values.astype(jnp.int32)


def shard_levels(rng, extent, shards, smallest, top_value):
    level, own = 1.0, jax.random.fold_in(rng, 6)
    for dim, blocks in shards:
        heights = jnp.exp(jax.random.uniform(jax.random.fold_in(own, dim), (blocks,), jnp.float32, smallest / len(shards), top_value / len(shards)))
        level = level * jnp.repeat(heights, extent[dim] // blocks).reshape([-1 if axis == dim else 1 for axis in range(len(extent))])
    return level


def gaussian(stream_key, shape, width, limit, cuts=(), kind=jnp.bfloat16):
    result = jax.random.normal(stream_key, shape, jnp.float32) * width
    if len(cuts) > 0:
        result = shard_levels(stream_key, shape, cuts, -0.22, 0.18) * result
    return jnp.clip(result, min=-limit, max=limit).astype(kind)


def setup_inputs(seed: int = 0) -> dict:
    key_list = jax.random.split(jax.random.key(seed), 8)
    return {
        "reference_scan": gaussian(key_list[0], (NEX, NEY, EZ * 512), 1.0, 6.0, ((0, 8), (1, 4))),
        "ref_gradient": gaussian(key_list[1], (3, NEX, NEY, EZ * 512), 1.0, 6.0, ((1, 8), (2, 4))),
        "deformed_scan": gaussian(key_list[2], (NEX, NEY, EZ * 512), 1.0, 6.0, ((0, 8), (1, 4))),
        "interp_weights": jnp.clip(1.0 * jax.random.uniform(key_list[3], (NEX, NEY, EZ * 512), jnp.float32) ** shard_levels(key_list[3], (NEX, NEY, EZ * 512), ((0, 8), (1, 4)), -0.2, 0.2), 0.0, 1.0).astype(jnp.bfloat16),
        "sample_mask": draw_sample_mask(jax.random.fold_in(key_list[7], 71), 0),
        "block_list": draw_block_list(jax.random.fold_in(key_list[7], 71), 0),
        "offsets": draw_offsets(jax.random.fold_in(key_list[7], 71), 0),
    }


tikhonov = 8.0


def shape_table():
    voxel = jnp.arange(512)
    coords = [((voxel // 64).astype(jnp.float32) + 0.5) / 8.0, (((voxel // 8) % 8).astype(jnp.float32) + 0.5) / 8.0, ((voxel % 8).astype(jnp.float32) + 0.5) / 8.0]
    rows = []
    for node in range(8):
        bits = [(node >> 2) & 1, (node >> 1) & 1, node & 1]
        value = jnp.ones((512,), jnp.float32)
        for axis_pos in range(3):
            value = value * (coords[axis_pos] if bits[axis_pos] else 1.0 - coords[axis_pos])
        rows.append(value)
    return jnp.transpose(jnp.stack(rows).reshape(8, 4, 128), (1, 0, 2))


def reference(reference_scan, ref_gradient, deformed_scan, interp_weights, sample_mask, block_list, offsets):
    margin = BOUND + 1
    total_x = EX * N_GX
    total_y = EY * N_GY
    padded = jnp.pad(deformed_scan, ((margin, margin), (margin, margin), (0, 0)))
    span_y = total_y + 2 * margin
    flat_scan = padded.reshape(-1, EZ, 512)
    pos_x = jnp.arange(total_x)[:, None, None]
    pos_y = jnp.arange(total_y)[None, :, None]
    source = (pos_x + offsets[0] + margin) * span_y + pos_y + offsets[1] + margin
    layer = jnp.broadcast_to(jnp.arange(EZ)[None, None, :], source.shape)
    near = flat_scan[source, layer].astype(jnp.float32)
    far = flat_scan[source + span_y, layer].astype(jnp.float32)
    weights = interp_weights.reshape(total_x, total_y, EZ, 512).astype(jnp.float32)
    warped = weights * near + (1.0 - weights) * far
    residual_image = (reference_scan.reshape(total_x, total_y, EZ, 512).astype(jnp.float32) - warped).astype(jnp.bfloat16)
    devices_total = N_GX * N_GY
    local_blocks = EX * EY * EZ * 4
    elements = EX * EY * EZ

    def to_devices(array):
        moved = jnp.transpose(array.reshape(N_GX, EX, N_GY, EY, EZ * 512), (0, 2, 1, 3, 4))
        return moved.reshape(devices_total, local_blocks, 128)

    resid_dev = to_devices(residual_image.reshape(total_x, total_y, EZ * 512))
    mask_dev = to_devices(sample_mask)
    grad_dev = jnp.stack([to_devices(ref_gradient[comp]) for comp in range(3)], axis=1)
    lists = block_list.reshape(devices_total, CAP)
    table = shape_table()

    def per_device(parts):
        grads, resid, mask, entries = parts
        listed = entries >= 0
        safe = jnp.maximum(entries, 0)
        shapes = table[safe % 4]
        grad_rows = jnp.moveaxis(grads[:, safe], 0, 1).astype(jnp.float32)
        product = (shapes[:, :, None, :] * grad_rows[:, None, :, :]).reshape(CAP, 24, 128)
        jacobian = lax.optimization_barrier(product.astype(jnp.bfloat16)).astype(jnp.float32)
        sampled = mask[safe].astype(jnp.float32) * listed[:, None].astype(jnp.float32)
        weighted = jacobian * sampled[:, None, :]
        hessian = jnp.einsum("bdv,bev->bde", weighted, jacobian, precision=lax.Precision.HIGHEST)
        gradient = jnp.einsum("bdv,bv->bd", weighted, resid[safe].astype(jnp.float32), precision=lax.Precision.HIGHEST)
        elem_hess = jnp.zeros((elements, 24, 24), jnp.float32).at[safe // 4].add(hessian)
        elem_load = jnp.zeros((elements, 24), jnp.float32).at[safe // 4].add(gradient)
        return elem_hess, elem_load

    elem_hess, elem_load = lax.map(per_device, (grad_dev, resid_dev, mask_dev, lists))
    stiffness = jnp.transpose(elem_hess.reshape(N_GX, N_GY, EX, EY, EZ, 24, 24), (0, 2, 1, 3, 4, 5, 6)).reshape(total_x, total_y, EZ, 24, 24)
    loads = jnp.transpose(elem_load.reshape(N_GX, N_GY, EX, EY, EZ, 24), (0, 2, 1, 3, 4, 5)).reshape(total_x, total_y, EZ, 24)

    def spread(field):
        wide = jnp.pad(field, ((0, 0), (0, 1), (0, 1), (0, 0)))
        pieces = []
        for node in range(8):
            i_bit, j_bit, l_bit = (node >> 2) & 1, (node >> 1) & 1, node & 1
            pieces.append(wide[:, i_bit:i_bit + total_x, j_bit:j_bit + total_y, l_bit:l_bit + EZ])
        stacked = jnp.stack(pieces)
        return jnp.transpose(stacked, (2, 3, 4, 0, 1)).reshape(total_x, total_y, EZ, 24)

    def collect(values):
        parts = jnp.transpose(values.reshape(total_x, total_y, EZ, 8, 3), (3, 4, 0, 1, 2))
        total = jnp.zeros((3, total_x + 1, total_y + 1, EZ + 1), jnp.float32)
        for node in range(8):
            i_bit, j_bit, l_bit = (node >> 2) & 1, (node >> 1) & 1, node & 1
            total = total + jnp.pad(parts[node], ((0, 0), (i_bit, 1 - i_bit), (j_bit, 1 - j_bit), (l_bit, 1 - l_bit)))
        return total[:, :total_x, :total_y]

    def operate(field):
        images = jnp.einsum("xyzde,xyze->xyzd", stiffness, spread(field), precision=lax.Precision.HIGHEST)
        return collect(images) + tikhonov * field

    rhs = collect(loads)
    increment = jnp.zeros_like(rhs)
    cg_residual = rhs
    direction = rhs
    norm_now = jnp.sum(cg_residual * cg_residual)
    for sweep in range(ITERS):
        image = operate(direction)
        step_size = norm_now / jnp.sum(direction * image)
        increment = increment + step_size * direction
        cg_residual = cg_residual - step_size * image
        norm_next = jnp.sum(cg_residual * cg_residual)
        direction = cg_residual + (norm_next / norm_now) * direction
        norm_now = norm_next
    return increment, cg_residual
```

```python
import functools

import jax
import jax.numpy as jnp
from jax import lax
from jax.experimental import pallas as pl
from jax.experimental.pallas import tpu as pltpu
from jax.sharding import PartitionSpec as P

BOUND = 4
ITERS = 3

tikhonov = 8.0

NODES = [(n >> 2 & 1, n >> 1 & 1, n & 1) for n in range(8)]
PAIRS = [(c, d) for c in range(3) for d in range(c, 3)]
PAIR_OF = {(c, d): PAIRS.index((min(c, d), max(c, d))) for c in range(3) for d in range(3)}
MESH = pl.DeviceIdType.MESH


def extended(value, axis, dim, before_width, after_width):
    devices, length = (lax.axis_size(axis), value.shape[dim])
    up = [(i, i + 1) for i in range(devices - 1)]
    down = [(j, i) for i, j in up]
    last = lax.slice_in_dim(value, length - before_width, length, axis=dim)
    first = lax.slice_in_dim(value, 0, after_width, axis=dim)
    before = lax.ppermute(last, axis, up)
    after = lax.ppermute(first, axis, down)
    return jnp.concatenate([before, value, after], axis=dim)


def split3(table):
    first = table.astype(jnp.bfloat16)
    rest = table - first.astype(jnp.float32)
    second = rest.astype(jnp.bfloat16)
    third = (rest - second.astype(jnp.float32)).astype(jnp.bfloat16)
    return [first, second, third]


def tables():
    voxel = jnp.arange(512)
    coords = [
        ((voxel // 64).astype(jnp.float32) + 0.5) / 8.0,
        ((voxel // 8 % 8).astype(jnp.float32) + 0.5) / 8.0,
        ((voxel % 8).astype(jnp.float32) + 0.5) / 8.0,
    ]
    linear = [[1.0 - t, t] for t in coords]
    quad = [[s[0] * s[0], s[0] * s[1], s[1] * s[1]] for s in linear]
    shapes = jnp.stack([linear[0][i] * linear[1][j] * linear[2][l] for i, j, l in NODES])
    squares = jnp.stack(
        [quad[0][a] * quad[1][b] * quad[2][c] for a in range(3) for b in range(3) for c in range(3)]
    )
    squares = jnp.pad(squares, ((0, 5), (0, 0)))
    square_table = jnp.concatenate(split3(squares), axis=0)
    shape_table = jnp.concatenate(split3(shapes) + [jnp.zeros((8, 512), jnp.bfloat16)], axis=0)
    return (square_table, shape_table)


def put_split(value, high_ref, low_ref, rows, lanes):
    high = value.astype(jnp.bfloat16)
    high_ref[rows, lanes] = high
    low_ref[rows, lanes] = (value - high.astype(jnp.float32)).astype(jnp.bfloat16)


def contract(table, part):
    return lax.dot_general(
        table, part, (((1,), (1,)), ((), ())), preferred_element_type=jnp.float32
    )


def hessian_kernel(depth, table_ref, grad_ref, mask_ref, out_ref, high_ref, low_ref):
    step = pl.program_id(0)
    tile_y = mask_ref.shape[1]
    wide = depth * tile_y
    for layer in range(depth):
        for chunk in range(4):
            source = pl.ds(layer * 512 + chunk * 128, 128)
            lanes = pl.ds(chunk * 128, 128)
            mask = mask_ref[0, :, source].astype(jnp.float32)
            grads = [grad_ref[c, 0, :, source].astype(jnp.float32) for c in range(3)]
            masked = [mask * g for g in grads]
            for q, (c, d) in enumerate(PAIRS):
                rows = pl.ds(q * wide + layer * tile_y, tile_y)
                put_split(masked[c] * grads[d], high_ref, low_ref, rows, lanes)
    table = table_ref[...]
    for q in range(6):
        rows = pl.ds(q * wide, wide)
        total = contract(table, high_ref[rows, :]) + contract(table, low_ref[rows, :])
        value = total[0:32] + total[32:64] + total[64:96]
        out_ref[q, :, pl.ds(step, 1), :] = value[:, None, :]


def load_kernel(
    depth,
    span_y,
    source_ref,
    table_ref,
    padded_ref,
    scan_ref,
    weight_ref,
    grad_ref,
    mask_ref,
    out_ref,
    wide_ref,
    near_ref,
    far_ref,
    high_ref,
    low_ref,
):
    step = pl.program_id(0)
    tile_y = mask_ref.shape[1]
    wide = depth * tile_y

    @pl.when(step == 0)
    def _():
        def convert(i, carry):
            wide_ref[pl.ds(pl.multiple_of(i * span_y, 8), span_y), :] = padded_ref[i].astype(
                jnp.float32
            )
            return carry

        lax.fori_loop(0, padded_ref.shape[0], convert, 0)

    def fetch(block, carry):
        for inner in range(4):
            y = block * 4 + inner
            for layer in range(depth):
                row = source_ref[(step * tile_y + y) * depth + layer]
                lanes = pl.ds(layer * 512, 512)
                near_ref[pl.ds(y, 1), lanes] = wide_ref[pl.ds(row, 1), lanes]
                far_ref[pl.ds(y, 1), lanes] = wide_ref[pl.ds(row + span_y, 1), lanes]
        return carry

    lax.fori_loop(0, tile_y // 4, fetch, 0)
    for layer in range(depth):
        for chunk in range(4):
            source = pl.ds(layer * 512 + chunk * 128, 128)
            lanes = pl.ds(chunk * 128, 128)
            weight = weight_ref[0, :, source].astype(jnp.float32)
            warped = weight * near_ref[:, source] + (1.0 - weight) * far_ref[:, source]
            image = scan_ref[0, :, source].astype(jnp.float32) - warped
            image = image.astype(jnp.bfloat16).astype(jnp.float32)
            image = image * mask_ref[0, :, source].astype(jnp.float32)
            for c in range(3):
                rows = pl.ds(c * wide + layer * tile_y, tile_y)
                value = image * grad_ref[c, 0, :, source].astype(jnp.float32)
                put_split(value, high_ref, low_ref, rows, lanes)
    table = table_ref[...]
    for c in range(3):
        rows = pl.ds(c * wide, wide)
        total = contract(table, high_ref[rows, :]) + contract(table, low_ref[rows, :])
        value = total[0:8] + total[8:16] + total[16:24]
        out_ref[c, :, pl.ds(step, 1), :] = value[:, None, :]


def solve_kernel(
    sizes,
    tile_y,
    hess_ref,
    load_ref,
    inc_ref,
    res_ref,
    field_ref,
    image_ref,
    out_x,
    out_y,
    out_c,
    in_x,
    in_y,
    in_c,
    own_x,
    got_x,
    own_y,
    got_y,
    send_sems,
    recv_sems,
    send_x,
    recv_x,
    send_y,
    recv_y,
):
    n_gx, n_gy = sizes
    tile_x, width = (hess_ref.shape[2], hess_ref.shape[3])
    gx = lax.axis_index("gx")
    gy = lax.axis_index("gy")
    in_x[...] = jnp.zeros_like(in_x)
    in_y[...] = jnp.zeros_like(in_y)
    in_c[...] = jnp.zeros_like(in_c)

    barrier = pltpu.get_barrier_semaphore()
    for k in range(1, n_gx):
        pl.semaphore_signal(barrier, inc=1, device_id=((gx + k) % n_gx, gy), device_id_type=MESH)
    for k in range(1, n_gy):
        pl.semaphore_signal(barrier, inc=1, device_id=(gx, (gy + k) % n_gy), device_id_type=MESH)
    low = jnp.logical_and(gx > 0, gy > 0)
    high = jnp.logical_and(gx < n_gx - 1, gy < n_gy - 1)

    @pl.when(low)
    def _():
        pl.semaphore_signal(barrier, inc=1, device_id=(gx - 1, gy - 1), device_id_type=MESH)

    @pl.when(high)
    def _():
        pl.semaphore_signal(barrier, inc=1, device_id=(gx + 1, gy + 1), device_id_type=MESH)

    corners = jnp.where(low, 1, 0) + jnp.where(high, 1, 0)
    pl.semaphore_wait(barrier, n_gx - 1 + n_gy - 1 + corners)

    lane = lax.broadcasted_iota(jnp.int32, (1, tile_x, width), 2)
    row = lax.broadcasted_iota(jnp.int32, (1, tile_x, width), 1)
    in_tile = lane % tile_y
    first_y = in_tile == 0
    last_y = in_tile == tile_y - 1
    first_x = row == 0
    last_x = row == tile_x - 1
    topmost = lane >= width - tile_y
    above = lane >= tile_y

    def copies(phase, dx, dy):
        def make(k, src, dst, target):
            return pltpu.make_async_remote_copy(
                src_ref=src.at[phase],
                dst_ref=dst.at[phase],
                send_sem=send_sems.at[phase, k],
                recv_sem=recv_sems.at[phase, k],
                device_id=target,
                device_id_type=MESH,
            )

        up = dx > 0
        send_gx, recv_gx = (gx < n_gx - 1, gx > 0) if up else (gx > 0, gx < n_gx - 1)
        send_gy, recv_gy = (gy < n_gy - 1, gy > 0) if up else (gy > 0, gy < n_gy - 1)
        return [
            (make(0, out_x, in_x, (gx + dx, gy)), send_gx, recv_gx),
            (make(1, out_y, in_y, (gx, gy + dy)), send_gy, recv_gy),
            (
                make(2, out_c, in_c, (gx + dx, gy + dy)),
                jnp.logical_and(send_gx, send_gy),
                jnp.logical_and(recv_gx, recv_gy),
            ),
        ]

    def start(phase, step):
        for copy, sends, _ in copies(phase, step, step):
            pl.when(sends)(copy.start)

    def arrive(phase, step):
        for copy, _, receives in copies(phase, step, step):
            pl.when(receives)(copy.wait_recv)

    def finish(phase, step):
        for copy, sends, _ in copies(phase, step, step):
            pl.when(sends)(copy.wait_send)

    def roll(value, shift, axis):
        return pltpu.roll(value, shift % value.shape[axis], axis)

    def shift_x(value):
        return jnp.where(first_x, 0.0, roll(value, 1, 1))

    def collect(phase):
        folded = {}
        for i in range(2):
            for j in range(2):
                under = image_ref[pl.ds((4 * i + 2 * j) * 3, 3)]
                over = image_ref[pl.ds((4 * i + 2 * j + 1) * 3, 3)]
                main = under + jnp.where(above, roll(over, tile_y, 2), 0.0)
                top = jnp.where(topmost, over, 0.0)
                folded[i, j] = jnp.concatenate([main, top], axis=0)
        kept, passed = ([], [])
        for i in range(2):
            kept.append(folded[i, 0] + jnp.where(first_y, 0.0, roll(folded[i, 1], 1, 2)))
            passed.append(jnp.where(first_y, roll(folded[i, 1], 1 - tile_y, 2), 0.0))
        out_x[phase] = kept[1][:, tile_x - 8 :, :]
        out_y[phase] = passed[0] + shift_x(passed[1])
        out_c[phase] = passed[1][:, tile_x - 8 :, :]
        start(phase, 1)
        total = kept[0] + shift_x(kept[1])
        arrive(phase, 1)
        edge = in_x[phase][:, 7:8, :] + in_c[phase][:, 7:8, :]
        return total + in_y[phase] + jnp.where(first_x, edge, 0.0)

    def spread(phase, field):
        turned = roll(field, tile_y - 1, 2)
        out_x[phase] = field[:, 0:8, :]
        out_y[phase] = turned
        out_c[phase] = turned[:, 0:8, :]
        start(phase, -1)
        next_x = roll(field, -1, 1)
        next_y = roll(field, -1, 2)

        def place(i, j, value):
            main, top = (value[0:3], value[3:6])
            field_ref[pl.ds((4 * i + 2 * j) * 3, 3)] = main
            field_ref[pl.ds((4 * i + 2 * j + 1) * 3, 3)] = jnp.where(
                topmost, top, roll(main, -tile_y, 2)
            )

        place(0, 0, field)
        arrive(phase, -1)
        side = in_x[phase]
        next_x = jnp.where(last_x, side[:, 0:1, :], next_x)
        next_y = jnp.where(last_y, in_y[phase], next_y)
        corner = jnp.where(last_y[:, 0:8], in_c[phase], roll(side, -1, 2))
        both = jnp.where(last_x, corner[:, 0:1, :], roll(next_y, -1, 1))
        place(1, 0, next_x)
        place(0, 1, next_y)
        place(1, 1, both)

    def apply():
        for n, (i, j, l) in enumerate(NODES):
            for c in range(3):
                total = None
                for m, (p, q, r) in enumerate(NODES):
                    kind = (i + p) * 9 + (j + q) * 3 + l + r
                    for d in range(3):
                        term = hess_ref[PAIR_OF[c, d], kind] * field_ref[3 * m + d]
                        total = term if total is None else total + term
                image_ref[3 * n + c] = total

    def reduce_over(own, got, sends, receives, slot, index, count, target):
        def make(k):
            return pltpu.make_async_remote_copy(
                src_ref=own.at[slot],
                dst_ref=got.at[slot, k - 1],
                send_sem=sends.at[slot, k - 1],
                recv_sem=receives.at[slot, k - 1],
                device_id=target((index + k) % count),
                device_id_type=MESH,
            )

        handles = [make(k) for k in range(1, count)]
        for copy in handles:
            copy.start()
        total = own[slot]
        for copy in handles:
            copy.wait_recv()
        for copy in handles:
            copy.wait_send()
        return total, [got[slot, k - 1] for k in range(1, count)]

    def in_order(index, count, mine, others):
        total = jnp.zeros_like(mine)
        for source in range(count):
            value = jnp.where(index == source, mine, 0.0)
            for k in range(1, count):
                value = jnp.where((index - k + count) % count == source, others[k - 1], value)
            total = total + value
        return total

    def two_products(slot, vector, image):
        one = jnp.sum(jnp.sum(vector * vector, axis=0), axis=0, keepdims=True)
        two = jnp.sum(jnp.sum(vector * image, axis=0), axis=0, keepdims=True)
        line = lax.broadcasted_iota(jnp.int32, (8, width), 0)
        own_x[slot] = jnp.where(line == 0, one, jnp.where(line == 1, two, 0.0))
        mine, others = reduce_over(
            own_x, got_x, send_x, recv_x, slot, gx, n_gx, lambda t: (t, gy)
        )
        own_y[slot] = in_order(gx, n_gx, mine, others)
        mine, others = reduce_over(
            own_y, got_y, send_y, recv_y, slot, gy, n_gy, lambda t: (gx, t)
        )
        total = in_order(gy, n_gy, mine, others)
        return (
            jnp.sum(total[0:1], axis=1, keepdims=True)[None],
            jnp.sum(total[1:2], axis=1, keepdims=True)[None],
        )

    def operate(phase, field):
        spread(phase, field)
        apply()
        return collect(phase + 1) + tikhonov * field

    for c in range(3):
        for n in range(8):
            image_ref[3 * n + c] = load_ref[c, n]
    rhs = collect(0)
    increment = jnp.zeros_like(rhs)
    residual = rhs
    image = operate(1, residual)
    norm_now, product = two_products(0, residual, image)
    step_size = norm_now / product
    direction, along = (residual, image)
    for sweep in range(ITERS):
        increment = increment + step_size * direction
        residual = residual - step_size * along
        if sweep + 1 < ITERS:
            image = operate(2 * sweep + 3, residual)
            norm_next, product = two_products(sweep + 1, residual, image)
            factor = norm_next / norm_now
            step_size = norm_next / (product - factor * norm_next / step_size)
            direction = residual + factor * direction
            along = image + factor * along
            norm_now = norm_next
    inc_ref[...] = increment
    res_ref[...] = residual
    finish(0, 1)
    for sweep in range(ITERS):
        finish(2 * sweep + 1, -1)
        finish(2 * sweep + 2, 1)


def per_device(
    reference_scan, ref_gradient, deformed_scan, interp_weights, sample_mask, block_list, offsets
):
    tile_x, tile_y, column = reference_scan.shape
    depth = column // 512
    width = depth * tile_y
    square_table, shape_table = tables()

    padded = extended(deformed_scan, "gx", 0, BOUND, BOUND + 1)
    padded = extended(padded, "gy", 1, BOUND, BOUND)
    span_x, span_y = padded.shape[:2]
    pos_x = jnp.arange(tile_x)[:, None, None]
    pos_y = jnp.arange(tile_y)[None, :, None]
    source = (pos_x + offsets[0] + BOUND) * span_y + pos_y + offsets[1] + BOUND

    voxels = pl.BlockSpec((1, tile_y, column), lambda x: (x, 0, 0))
    gradients = pl.BlockSpec((3, 1, tile_y, column), lambda x: (0, x, 0, 0))
    vmem = pl.BlockSpec(memory_space=pltpu.VMEM)
    size = tile_x * tile_y * column
    hessian = pl.pallas_call(
        functools.partial(hessian_kernel, depth),
        grid=(tile_x,),
        out_shape=jax.ShapeDtypeStruct((6, 32, tile_x, width), jnp.float32),
        in_specs=[pl.BlockSpec((96, 512), lambda x: (0, 0)), gradients, voxels],
        out_specs=pl.BlockSpec((6, 32, tile_x, width), lambda x: (0, 0, 0, 0)),
        scratch_shapes=[pltpu.VMEM((6 * width, 512), jnp.bfloat16)] * 2,
        cost_estimate=pl.CostEstimate(
            flops=size * 6 * 2 * 256, bytes_accessed=size * 10, transcendentals=0
        ),
        name="hessian",
    )(square_table, ref_gradient, sample_mask)
    load = pl.pallas_call(
        functools.partial(load_kernel, depth, span_y),
        grid=(tile_x,),
        out_shape=jax.ShapeDtypeStruct((3, 8, tile_x, width), jnp.float32),
        in_specs=[
            pl.BlockSpec(memory_space=pltpu.SMEM),
            pl.BlockSpec((32, 512), lambda x: (0, 0)),
            pl.BlockSpec((span_x, span_y, column), lambda x: (0, 0, 0)),
            voxels,
            voxels,
            gradients,
            voxels,
        ],
        out_specs=pl.BlockSpec((3, 8, tile_x, width), lambda x: (0, 0, 0, 0)),
        scratch_shapes=[
            pltpu.VMEM((span_x * span_y, column), jnp.float32),
            pltpu.VMEM((tile_y, column), jnp.float32),
            pltpu.VMEM((tile_y, column), jnp.float32),
            pltpu.VMEM((3 * width, 512), jnp.bfloat16),
            pltpu.VMEM((3 * width, 512), jnp.bfloat16),
        ],
        name="load",
    )(
        source.reshape(-1),
        shape_table,
        padded,
        reference_scan,
        interp_weights,
        ref_gradient,
        sample_mask,
    )
    n_gx, n_gy = (lax.axis_size("gx"), lax.axis_size("gy"))
    phases = 2 * ITERS + 1
    part = jax.ShapeDtypeStruct((6, tile_x, width), jnp.float32)
    dma = pltpu.SemaphoreType.DMA
    increment, residual = pl.pallas_call(
        functools.partial(solve_kernel, (n_gx, n_gy), tile_y),
        out_shape=(part, part),
        in_specs=[vmem, vmem],
        out_specs=(vmem, vmem),
        scratch_shapes=[
            pltpu.VMEM((24, tile_x, width), jnp.float32),
            pltpu.VMEM((24, tile_x, width), jnp.float32),
        ]
        + [
            pltpu.VMEM((phases, 6, rows, width), jnp.float32)
            for rows in (8, tile_x, 8, 8, tile_x, 8)
        ]
        + [
            pltpu.VMEM((ITERS, 8, width), jnp.float32),
            pltpu.VMEM((ITERS, n_gx - 1, 8, width), jnp.float32),
            pltpu.VMEM((ITERS, 8, width), jnp.float32),
            pltpu.VMEM((ITERS, n_gy - 1, 8, width), jnp.float32),
            dma((phases, 3)),
            dma((phases, 3)),
            dma((ITERS, n_gx - 1)),
            dma((ITERS, n_gx - 1)),
            dma((ITERS, n_gy - 1)),
            dma((ITERS, n_gy - 1)),
        ],
        compiler_params=pltpu.CompilerParams(collective_id=0, has_side_effects=True),
        name="solve",
    )(hessian, load)

    def nodal(value):
        main = jnp.transpose(value[:3].reshape(3, tile_x, depth, tile_y), (0, 1, 3, 2))
        return jnp.concatenate([main, value[3:, :, width - tile_y :, None]], axis=3)

    return (nodal(increment), nodal(residual))


def solution(mesh):
    return jax.shard_map(
        per_device,
        mesh=mesh,
        in_specs=(
            P("gx", "gy", None),
            P(None, "gx", "gy", None),
            P("gx", "gy", None),
            P("gx", "gy", None),
            P("gx", "gy", None),
            P("gx", "gy"),
            P(None, "gx", "gy", None),
        ),
        out_specs=(P(None, "gx", "gy", None), P(None, "gx", "gy", None)),
        check_vma=False,
    )
```

```python
import functools

import jax
import jax.numpy as jnp
from jax import lax
from jax.experimental import pallas as pl
from jax.experimental.pallas import tpu as pltpu
from jax.sharding import PartitionSpec as P


BOUND = 4
ITERS = 3

tikhonov = 8.0

NODES = [(n >> 2 & 1, n >> 1 & 1, n & 1) for n in range(8)]
PAIRS = [(c, d) for c in range(3) for d in range(c, 3)]
PAIR_OF = {(c, d): PAIRS.index((min(c, d), max(c, d))) for c in range(3) for d in range(3)}
MESH = pl.DeviceIdType.MESH


def shifted(block, dx, dy):
    n_gx, n_gy = (lax.axis_size("gx"), lax.axis_size("gy"))
    route = [
        (i * n_gy + j, (i + dx) * n_gy + j + dy)
        for i in range(n_gx)
        for j in range(n_gy)
        if 0 <= i + dx < n_gx and 0 <= j + dy < n_gy
    ]
    return lax.ppermute(block, ("gx", "gy"), route)


def surroundings(scan):
    rows = [scan[-BOUND:], scan, scan[: BOUND + 1]]
    pieces = []
    for block, dx in zip(rows, (1, 0, -1)):
        pieces.append(shifted(block, dx, 0) if dx else block)
        beyond = shifted(block[:, :BOUND], dx, -1)
        ahead = shifted(block[:, -BOUND:], dx, 1)
        pieces.append(jnp.concatenate([beyond, ahead], axis=1))
    return pieces


def split3(table):
    first = table.astype(jnp.bfloat16)
    rest = table - first.astype(jnp.float32)
    second = rest.astype(jnp.bfloat16)
    third = (rest - second.astype(jnp.float32)).astype(jnp.bfloat16)
    return [first, second, third]


def tables():
    voxel = jnp.arange(512)
    coords = [
        ((voxel // 64).astype(jnp.float32) + 0.5) / 8.0,
        ((voxel // 8 % 8).astype(jnp.float32) + 0.5) / 8.0,
        ((voxel % 8).astype(jnp.float32) + 0.5) / 8.0,
    ]
    linear = [[1.0 - t, t] for t in coords]
    quad = [[s[0] * s[0], s[0] * s[1], s[1] * s[1]] for s in linear]
    shapes = jnp.stack([linear[0][i] * linear[1][j] * linear[2][l] for i, j, l in NODES])
    squares = jnp.stack(
        [quad[0][a] * quad[1][b] * quad[2][c] for a in range(3) for b in range(3) for c in range(3)]
    )
    squares = jnp.pad(squares, ((0, 5), (0, 0)))
    square_table = jnp.concatenate(split3(squares), axis=0)
    shape_table = jnp.concatenate(split3(shapes) + [jnp.zeros((8, 512), jnp.bfloat16)], axis=0)
    return (square_table, shape_table)


def put_split(value, high_ref, low_ref, rows, lanes):
    high = value.astype(jnp.bfloat16)
    high_ref[rows, lanes] = high
    low_ref[rows, lanes] = (value - high.astype(jnp.float32)).astype(jnp.bfloat16)


def contract(table, part):
    return lax.dot_general(
        table, part, (((1,), (1,)), ((), ())), preferred_element_type=jnp.float32
    )


def hessian_kernel(depth, table_ref, grad_ref, mask_ref, out_ref, high_ref, low_ref):
    step = pl.program_id(0)
    tile_y = mask_ref.shape[1]
    wide = depth * tile_y
    for layer in range(depth):
        for chunk in range(4):
            source = pl.ds(layer * 512 + chunk * 128, 128)
            lanes = pl.ds(chunk * 128, 128)
            mask = mask_ref[0, :, source].astype(jnp.float32)
            grads = [grad_ref[c, 0, :, source].astype(jnp.float32) for c in range(3)]
            masked = [mask * g for g in grads]
            for q, (c, d) in enumerate(PAIRS):
                rows = pl.ds(q * wide + layer * tile_y, tile_y)
                put_split(masked[c] * grads[d], high_ref, low_ref, rows, lanes)
    table = table_ref[...]
    for q in range(6):
        rows = pl.ds(q * wide, wide)
        total = contract(table, high_ref[rows, :]) + contract(table, low_ref[rows, :])
        value = total[0:32] + total[32:64] + total[64:96]
        out_ref[q, :, pl.ds(step, 1), :] = value[:, None, :]


def load_kernel(
    depth,
    span_y,
    source_ref,
    table_ref,
    *refs,
):
    piece_refs = refs[:6]
    scan_ref, weight_ref, grad_ref, mask_ref, out_ref = refs[6:11]
    wide_ref, near_ref, far_ref, high_ref, low_ref = refs[11:]
    step = pl.program_id(0)
    tile_y = mask_ref.shape[1]
    wide = depth * tile_y

    @pl.when(step == 0)
    def _():
        begin = 0
        for band in range(3):
            middle, sides = piece_refs[2 * band : 2 * band + 2]

            def convert(i, carry, begin=begin, middle=middle, sides=sides):
                base = pl.multiple_of((begin + i) * span_y, 8)
                wide_ref[pl.ds(base, tile_y), :] = middle[i].astype(jnp.float32)
                wide_ref[pl.ds(base + tile_y, 2 * BOUND), :] = sides[i].astype(jnp.float32)
                return carry

            lax.fori_loop(0, middle.shape[0], convert, 0)
            begin += middle.shape[0]

    def fetch(block, carry):
        for inner in range(4):
            y = block * 4 + inner
            for layer in range(depth):
                row = source_ref[(step * tile_y + y) * depth + layer]
                lanes = pl.ds(layer * 512, 512)
                near_ref[pl.ds(y, 1), lanes] = wide_ref[pl.ds(row, 1), lanes]
                far_ref[pl.ds(y, 1), lanes] = wide_ref[pl.ds(row + span_y, 1), lanes]
        return carry

    lax.fori_loop(0, tile_y // 4, fetch, 0)
    for layer in range(depth):
        for chunk in range(4):
            source = pl.ds(layer * 512 + chunk * 128, 128)
            lanes = pl.ds(chunk * 128, 128)
            weight = weight_ref[0, :, source].astype(jnp.float32)
            warped = weight * near_ref[:, source] + (1.0 - weight) * far_ref[:, source]
            image = scan_ref[0, :, source].astype(jnp.float32) - warped
            image = image.astype(jnp.bfloat16).astype(jnp.float32)
            image = image * mask_ref[0, :, source].astype(jnp.float32)
            for c in range(3):
                rows = pl.ds(c * wide + layer * tile_y, tile_y)
                value = image * grad_ref[c, 0, :, source].astype(jnp.float32)
                put_split(value, high_ref, low_ref, rows, lanes)
    table = table_ref[...]
    for c in range(3):
        rows = pl.ds(c * wide, wide)
        total = contract(table, high_ref[rows, :]) + contract(table, low_ref[rows, :])
        value = total[0:8] + total[8:16] + total[16:24]
        out_ref[c, :, pl.ds(step, 1), :] = value[:, None, :]


def solve_kernel(
    sizes,
    tile_y,
    hess_ref,
    load_ref,
    inc_ref,
    res_ref,
    field_ref,
    image_ref,
    out_x,
    out_y,
    out_c,
    in_x,
    in_y,
    in_c,
    own_x,
    got_x,
    own_y,
    got_y,
    send_sems,
    recv_sems,
    send_x,
    recv_x,
    send_y,
    recv_y,
):
    n_gx, n_gy = sizes
    tile_x, width = (hess_ref.shape[2], hess_ref.shape[3])
    gx = lax.axis_index("gx")
    gy = lax.axis_index("gy")
    in_x[...] = jnp.zeros_like(in_x)
    in_y[...] = jnp.zeros_like(in_y)
    in_c[...] = jnp.zeros_like(in_c)

    barrier = pltpu.get_barrier_semaphore()
    for k in range(1, n_gx):
        pl.semaphore_signal(barrier, inc=1, device_id=((gx + k) % n_gx, gy), device_id_type=MESH)
    for k in range(1, n_gy):
        pl.semaphore_signal(barrier, inc=1, device_id=(gx, (gy + k) % n_gy), device_id_type=MESH)
    low = jnp.logical_and(gx > 0, gy > 0)
    high = jnp.logical_and(gx < n_gx - 1, gy < n_gy - 1)

    @pl.when(low)
    def _():
        pl.semaphore_signal(barrier, inc=1, device_id=(gx - 1, gy - 1), device_id_type=MESH)

    @pl.when(high)
    def _():
        pl.semaphore_signal(barrier, inc=1, device_id=(gx + 1, gy + 1), device_id_type=MESH)

    corners = jnp.where(low, 1, 0) + jnp.where(high, 1, 0)
    pl.semaphore_wait(barrier, n_gx - 1 + n_gy - 1 + corners)

    lane = lax.broadcasted_iota(jnp.int32, (1, tile_x, width), 2)
    row = lax.broadcasted_iota(jnp.int32, (1, tile_x, width), 1)
    in_tile = lane % tile_y
    first_y = in_tile == 0
    last_y = in_tile == tile_y - 1
    first_x = row == 0
    last_x = row == tile_x - 1
    topmost = lane >= width - tile_y
    above = lane >= tile_y

    def copies(phase, dx, dy):
        def make(k, src, dst, target):
            return pltpu.make_async_remote_copy(
                src_ref=src.at[phase],
                dst_ref=dst.at[phase],
                send_sem=send_sems.at[phase, k],
                recv_sem=recv_sems.at[phase, k],
                device_id=target,
                device_id_type=MESH,
            )

        up = dx > 0
        send_gx, recv_gx = (gx < n_gx - 1, gx > 0) if up else (gx > 0, gx < n_gx - 1)
        send_gy, recv_gy = (gy < n_gy - 1, gy > 0) if up else (gy > 0, gy < n_gy - 1)
        return [
            (make(0, out_x, in_x, (gx + dx, gy)), send_gx, recv_gx),
            (make(1, out_y, in_y, (gx, gy + dy)), send_gy, recv_gy),
            (
                make(2, out_c, in_c, (gx + dx, gy + dy)),
                jnp.logical_and(send_gx, send_gy),
                jnp.logical_and(recv_gx, recv_gy),
            ),
        ]

    def start(phase, step):
        for copy, sends, _ in copies(phase, step, step):
            pl.when(sends)(copy.start)

    def arrive(phase, step):
        for copy, _, receives in copies(phase, step, step):
            pl.when(receives)(copy.wait_recv)

    def finish(phase, step):
        for copy, sends, _ in copies(phase, step, step):
            pl.when(sends)(copy.wait_send)

    def roll(value, shift, axis):
        return pltpu.roll(value, shift % value.shape[axis], axis)

    def shift_x(value):
        return jnp.where(first_x, 0.0, roll(value, 1, 1))

    def collect(phase, meanwhile):
        folded = {}
        for i in range(2):
            for j in range(2):
                under = image_ref[pl.ds((4 * i + 2 * j) * 3, 3)]
                over = image_ref[pl.ds((4 * i + 2 * j + 1) * 3, 3)]
                main = under + jnp.where(above, roll(over, tile_y, 2), 0.0)
                top = jnp.where(topmost, over, 0.0)
                folded[i, j] = jnp.concatenate([main, top], axis=0)
        kept, passed = ([], [])
        for i in range(2):
            kept.append(folded[i, 0] + jnp.where(first_y, 0.0, roll(folded[i, 1], 1, 2)))
            passed.append(jnp.where(first_y, roll(folded[i, 1], 1 - tile_y, 2), 0.0))
        out_x[phase] = kept[1][:, tile_x - 8 :, :]
        out_y[phase] = passed[0] + shift_x(passed[1])
        out_c[phase] = passed[1][:, tile_x - 8 :, :]
        start(phase, 1)
        total = kept[0] + shift_x(kept[1])
        meanwhile()
        arrive(phase, 1)
        edge = in_x[phase][:, 7:8, :] + in_c[phase][:, 7:8, :]
        return total + in_y[phase] + jnp.where(first_x, edge, 0.0)

    def spread(phase, field, meanwhile):
        turned = roll(field, tile_y - 1, 2)
        out_x[phase] = field[:, 0:8, :]
        out_y[phase] = turned
        out_c[phase] = turned[:, 0:8, :]
        start(phase, -1)
        meanwhile()
        next_x = roll(field, -1, 1)
        next_y = roll(field, -1, 2)

        def place(i, j, value):
            main, top = (value[0:3], value[3:6])
            field_ref[pl.ds((4 * i + 2 * j) * 3, 3)] = main
            field_ref[pl.ds((4 * i + 2 * j + 1) * 3, 3)] = jnp.where(
                topmost, top, roll(main, -tile_y, 2)
            )

        place(0, 0, field)
        arrive(phase, -1)
        side = in_x[phase]
        next_x = jnp.where(last_x, side[:, 0:1, :], next_x)
        next_y = jnp.where(last_y, in_y[phase], next_y)
        corner = jnp.where(last_y[:, 0:8], in_c[phase], roll(side, -1, 2))
        both = jnp.where(last_x, corner[:, 0:1, :], roll(next_y, -1, 1))
        place(1, 0, next_x)
        place(0, 1, next_y)
        place(1, 1, both)

    def apply():
        for n, (i, j, l) in enumerate(NODES):
            for c in range(3):
                total = None
                for m, (p, q, r) in enumerate(NODES):
                    kind = (i + p) * 9 + (j + q) * 3 + l + r
                    for d in range(3):
                        term = hess_ref[PAIR_OF[c, d], kind] * field_ref[3 * m + d]
                        total = term if total is None else total + term
                image_ref[3 * n + c] = total

    def exchange(own, got, sends, receives, slot, index, count, target):
        return [
            pltpu.make_async_remote_copy(
                src_ref=own.at[slot],
                dst_ref=got.at[slot, k - 1],
                send_sem=sends.at[slot, k - 1],
                recv_sem=receives.at[slot, k - 1],
                device_id=target((index + k) % count),
                device_id_type=MESH,
            )
            for k in range(1, count)
        ]

    def along_x(slot):
        return exchange(own_x, got_x, send_x, recv_x, slot, gx, n_gx, lambda t: (t, gy))

    def along_y(slot):
        return exchange(own_y, got_y, send_y, recv_y, slot, gy, n_gy, lambda t: (gx, t))

    def total_of(copies, own, got, slot, index, count):
        for copy in copies:
            copy.wait_recv()
        others = [got[slot, k - 1] for k in range(1, count)]
        return in_order(index, count, own[slot], others)

    def in_order(index, count, mine, others):
        total = jnp.zeros_like(mine)
        for source in range(count):
            value = jnp.where(index == source, mine, 0.0)
            for k in range(1, count):
                value = jnp.where((index - k + count) % count == source, others[k - 1], value)
            total = total + value
        return total

    def open_products(slot, vector, image):
        one = jnp.sum(jnp.sum(vector * vector, axis=0), axis=0, keepdims=True)
        two = jnp.sum(jnp.sum(vector * image, axis=0), axis=0, keepdims=True)
        line = lax.broadcasted_iota(jnp.int32, (8, width), 0)
        own_x[slot] = jnp.where(line == 0, one, jnp.where(line == 1, two, 0.0))
        for copy in along_x(slot):
            copy.start()

    def pass_products(slot):
        own_y[slot] = total_of(along_x(slot), own_x, got_x, slot, gx, n_gx)
        for copy in along_y(slot):
            copy.start()

    def close_products(slot):
        total = total_of(along_y(slot), own_y, got_y, slot, gy, n_gy)
        return (
            jnp.sum(total[0:1], axis=1, keepdims=True)[None],
            jnp.sum(total[1:2], axis=1, keepdims=True)[None],
        )

    def nothing():
        return None

    def operate(phase, field, during_spread=nothing, during_collect=nothing):
        spread(phase, field, during_spread)
        apply()
        return collect(phase + 1, during_collect) + tikhonov * field

    for c in range(3):
        for n in range(8):
            image_ref[3 * n + c] = load_ref[c, n]
    rhs = collect(0, nothing)
    increment = jnp.zeros_like(rhs)
    residual = rhs
    image = operate(1, residual)
    for sweep in range(ITERS):
        if sweep + 1 < ITERS:
            second = operate(
                2 * sweep + 3,
                image,
                lambda: open_products(sweep, residual, image),
                lambda: pass_products(sweep),
            )
        else:
            open_products(sweep, residual, image)
            pass_products(sweep)
        norm_next, product = close_products(sweep)
        if sweep == 0:
            step_size = norm_next / product
            direction, along = (residual, image)
        else:
            factor = norm_next / norm_now
            step_size = norm_next / (product - factor * norm_next / step_size)
            direction = residual + factor * direction
            along = image + factor * along
        norm_now = norm_next
        increment = increment + step_size * direction
        residual = residual - step_size * along
        if sweep + 1 < ITERS:
            deep = second if sweep == 0 else second + factor * deep
            image = image - step_size * deep
    inc_ref[...] = increment
    res_ref[...] = residual
    finish(0, 1)
    for sweep in range(ITERS):
        finish(2 * sweep + 1, -1)
        finish(2 * sweep + 2, 1)
        for copy in along_x(sweep) + along_y(sweep):
            copy.wait_send()


def per_device(
    reference_scan, ref_gradient, deformed_scan, interp_weights, sample_mask, block_list, offsets
):
    tile_x, tile_y, column = reference_scan.shape
    depth = column // 512
    width = depth * tile_y
    square_table, shape_table = tables()

    pieces = surroundings(deformed_scan)
    span_x, span_y = (tile_x + 2 * BOUND + 1, tile_y + 2 * BOUND)
    pos_x = jnp.arange(tile_x)[:, None, None]
    pos_y = jnp.arange(tile_y)[None, :, None]
    source = (pos_x + offsets[0] + BOUND) * span_y + (pos_y + offsets[1] + span_y) % span_y

    voxels = pl.BlockSpec((1, tile_y, column), lambda x: (x, 0, 0))
    gradients = pl.BlockSpec((3, 1, tile_y, column), lambda x: (0, x, 0, 0))
    vmem = pl.BlockSpec(memory_space=pltpu.VMEM)
    size = tile_x * tile_y * column
    hessian = pl.pallas_call(
        functools.partial(hessian_kernel, depth),
        grid=(tile_x,),
        out_shape=jax.ShapeDtypeStruct((6, 32, tile_x, width), jnp.float32),
        in_specs=[pl.BlockSpec((96, 512), lambda x: (0, 0)), gradients, voxels],
        out_specs=pl.BlockSpec((6, 32, tile_x, width), lambda x: (0, 0, 0, 0)),
        scratch_shapes=[pltpu.VMEM((6 * width, 512), jnp.bfloat16)] * 2,
        cost_estimate=pl.CostEstimate(
            flops=size * 6 * 2 * 256, bytes_accessed=size * 10, transcendentals=0
        ),
        name="hessian",
    )(square_table, ref_gradient, sample_mask)
    load = pl.pallas_call(
        functools.partial(load_kernel, depth, span_y),
        grid=(tile_x,),
        out_shape=jax.ShapeDtypeStruct((3, 8, tile_x, width), jnp.float32),
        in_specs=[
            pl.BlockSpec(memory_space=pltpu.SMEM),
            pl.BlockSpec((32, 512), lambda x: (0, 0)),
        ]
        + [pl.BlockSpec(piece.shape, lambda x: (0, 0, 0)) for piece in pieces]
        + [
            voxels,
            voxels,
            gradients,
            voxels,
        ],
        out_specs=pl.BlockSpec((3, 8, tile_x, width), lambda x: (0, 0, 0, 0)),
        scratch_shapes=[
            pltpu.VMEM((span_x * span_y, column), jnp.float32),
            pltpu.VMEM((tile_y, column), jnp.float32),
            pltpu.VMEM((tile_y, column), jnp.float32),
            pltpu.VMEM((3 * width, 512), jnp.bfloat16),
            pltpu.VMEM((3 * width, 512), jnp.bfloat16),
        ],
        name="load",
    )(
        source.reshape(-1),
        shape_table,
        *pieces,
        reference_scan,
        interp_weights,
        ref_gradient,
        sample_mask,
    )
    n_gx, n_gy = (lax.axis_size("gx"), lax.axis_size("gy"))
    phases = 2 * ITERS + 1
    part = jax.ShapeDtypeStruct((6, tile_x, width), jnp.float32)
    dma = pltpu.SemaphoreType.DMA
    increment, residual = pl.pallas_call(
        functools.partial(solve_kernel, (n_gx, n_gy), tile_y),
        out_shape=(part, part),
        in_specs=[vmem, vmem],
        out_specs=(vmem, vmem),
        scratch_shapes=[
            pltpu.VMEM((24, tile_x, width), jnp.float32),
            pltpu.VMEM((24, tile_x, width), jnp.float32),
        ]
        + [
            pltpu.VMEM((phases, 6, rows, width), jnp.float32)
            for rows in (8, tile_x, 8, 8, tile_x, 8)
        ]
        + [
            pltpu.VMEM((ITERS, 8, width), jnp.float32),
            pltpu.VMEM((ITERS, n_gx - 1, 8, width), jnp.float32),
            pltpu.VMEM((ITERS, 8, width), jnp.float32),
            pltpu.VMEM((ITERS, n_gy - 1, 8, width), jnp.float32),
            dma((phases, 3)),
            dma((phases, 3)),
            dma((ITERS, n_gx - 1)),
            dma((ITERS, n_gx - 1)),
            dma((ITERS, n_gy - 1)),
            dma((ITERS, n_gy - 1)),
        ],
        compiler_params=pltpu.CompilerParams(collective_id=0, has_side_effects=True),
        name="solve",
    )(hessian, load)

    def nodal(value):
        main = jnp.transpose(value[:3].reshape(3, tile_x, depth, tile_y), (0, 1, 3, 2))
        return jnp.concatenate([main, value[3:, :, width - tile_y :, None]], axis=3)

    return (nodal(increment), nodal(residual))


def solution(mesh):
    return jax.shard_map(
        per_device,
        mesh=mesh,
        in_specs=(
            P("gx", "gy", None),
            P(None, "gx", "gy", None),
            P("gx", "gy", None),
            P("gx", "gy", None),
            P("gx", "gy", None),
            P("gx", "gy"),
            P(None, "gx", "gy", None),
        ),
        out_specs=(P(None, "gx", "gy", None), P(None, "gx", "gy", None)),
        check_vma=False,
    )
```

```python
import functools

import jax
import jax.numpy as jnp
from jax import lax
from jax.experimental import pallas as pl
from jax.experimental.pallas import tpu as pltpu
from jax.sharding import PartitionSpec as P

BOUND = 4
ITERS = 3

tikhonov = 8.0

NODES = [(n >> 2 & 1, n >> 1 & 1, n & 1) for n in range(8)]
PAIRS = [(c, d) for c in range(3) for d in range(c, 3)]
PAIR_OF = {(c, d): PAIRS.index((min(c, d), max(c, d))) for c in range(3) for d in range(3)}
MESH = pl.DeviceIdType.MESH


def split3(table):
    first = table.astype(jnp.bfloat16)
    rest = table - first.astype(jnp.float32)
    second = rest.astype(jnp.bfloat16)
    third = (rest - second.astype(jnp.float32)).astype(jnp.bfloat16)
    return [first, second, third]


def tables():
    voxel = jnp.arange(512)
    coords = [
        ((voxel // 64).astype(jnp.float32) + 0.5) / 8.0,
        ((voxel // 8 % 8).astype(jnp.float32) + 0.5) / 8.0,
        ((voxel % 8).astype(jnp.float32) + 0.5) / 8.0,
    ]
    linear = [[1.0 - t, t] for t in coords]
    quad = [[s[0] * s[0], s[0] * s[1], s[1] * s[1]] for s in linear]
    shapes = jnp.stack([linear[0][i] * linear[1][j] * linear[2][l] for i, j, l in NODES])
    squares = jnp.stack(
        [quad[0][a] * quad[1][b] * quad[2][c] for a in range(3) for b in range(3) for c in range(3)]
    )
    squares = jnp.pad(squares, ((0, 5), (0, 0)))
    square_table = jnp.concatenate(split3(squares), axis=0)
    shape_table = jnp.concatenate(split3(shapes) + [jnp.zeros((8, 512), jnp.bfloat16)], axis=0)
    return (square_table, shape_table)


def put_split(value, high_ref, low_ref, rows, lanes):
    high = value.astype(jnp.bfloat16)
    high_ref[rows, lanes] = high
    low_ref[rows, lanes] = (value - high.astype(jnp.float32)).astype(jnp.bfloat16)


def contract(table, part):
    return lax.dot_general(
        table, part, (((1,), (1,)), ((), ())), preferred_element_type=jnp.float32
    )


def hessian_kernel(
    depth,
    sizes,
    table_ref,
    grad_ref,
    mask_ref,
    scan_ref,
    out_ref,
    before_ref,
    after_ref,
    beyond_ref,
    ahead_ref,
    high_ref,
    low_ref,
    send_sems,
    recv_sems,
):
    step = pl.program_id(0)
    tile_y = mask_ref.shape[1]
    tile_x = scan_ref.shape[0]
    gx = lax.axis_index("gx")
    gy = lax.axis_index("gy")
    not_first_x, not_last_x = (gx > 0, gx < sizes[0] - 1)
    not_first_y, not_last_y = (gy > 0, gy < sizes[1] - 1)
    both = jnp.logical_and

    def copy(k, source, target, device):
        return pltpu.make_async_remote_copy(
            src_ref=source,
            dst_ref=target,
            send_sem=send_sems.at[k],
            recv_sem=recv_sems.at[k],
            device_id=device,
            device_id_type=MESH,
        )

    every, low_y, high_y = (slice(None), pl.ds(0, 8), pl.ds(tile_y - 8, 8))
    own = pl.ds(BOUND, tile_x)
    front, back = (pl.ds(0, BOUND), pl.ds(BOUND + tile_x, BOUND + 1))
    near_y, far_y = ((gx, gy - 1), (gx, gy + 1))
    direct = [
        (
            copy(0, scan_ref.at[pl.ds(tile_x - BOUND, BOUND)], before_ref, (gx + 1, gy)),
            not_last_x,
            not_first_x,
        ),
        (
            copy(1, scan_ref.at[pl.ds(0, BOUND + 1)], after_ref, (gx - 1, gy)),
            not_first_x,
            not_last_x,
        ),
        (
            copy(2, scan_ref.at[every, low_y], beyond_ref.at[own], near_y),
            not_first_y,
            not_last_y,
        ),
        (
            copy(3, scan_ref.at[every, high_y], ahead_ref.at[own], far_y),
            not_last_y,
            not_first_y,
        ),
    ]
    forwarded = []
    for k, band, rows, present in (
        (4, before_ref, front, not_first_x),
        (6, after_ref, back, not_last_x),
    ):
        forwarded.append(
            (
                copy(k, band.at[every, low_y], beyond_ref.at[rows], near_y),
                both(present, not_first_y),
                both(present, not_last_y),
            )
        )
        forwarded.append(
            (
                copy(k + 1, band.at[every, high_y], ahead_ref.at[rows], far_y),
                both(present, not_last_y),
                both(present, not_first_y),
            )
        )

    @pl.when(step == 0)
    def _():
        barrier = pltpu.get_barrier_semaphore()
        peers = 0
        for present, device in (
            (not_first_x, (gx - 1, gy)),
            (not_last_x, (gx + 1, gy)),
            (not_first_y, near_y),
            (not_last_y, far_y),
        ):
            peers = peers + jnp.where(present, 1, 0)

            @pl.when(present)
            def _(device=device):
                pl.semaphore_signal(barrier, inc=1, device_id=device, device_id_type=MESH)

        pl.semaphore_wait(barrier, peers)
        for one, sends, _ in direct:
            pl.when(sends)(one.start)

    wide = depth * tile_y
    for layer in range(depth):
        for chunk in range(4):
            source = pl.ds(layer * 512 + chunk * 128, 128)
            lanes = pl.ds(chunk * 128, 128)
            mask = mask_ref[0, :, source].astype(jnp.float32)
            grads = [grad_ref[c, 0, :, source].astype(jnp.float32) for c in range(3)]
            masked = [mask * g for g in grads]
            for q, (c, d) in enumerate(PAIRS):
                rows = pl.ds(q * wide + layer * tile_y, tile_y)
                put_split(masked[c] * grads[d], high_ref, low_ref, rows, lanes)
    table = table_ref[...]
    for q in range(6):
        rows = pl.ds(q * wide, wide)
        total = contract(table, high_ref[rows, :]) + contract(table, low_ref[rows, :])
        value = total[0:32] + total[32:64] + total[64:96]
        out_ref[q, :, pl.ds(step, 1), :] = value[:, None, :]

    @pl.when(step == tile_x - 1)
    def _():
        for k in range(2):
            one, _, receives = direct[k]
            pl.when(receives)(one.wait_recv)
            for other, sends, _ in forwarded[2 * k : 2 * k + 2]:
                pl.when(sends)(other.start)
        for one, _, receives in direct[2:] + forwarded:
            pl.when(receives)(one.wait_recv)
        for one, sends, _ in direct + forwarded:
            pl.when(sends)(one.wait_send)


def load_kernel(
    depth,
    span_y,
    sizes,
    source_ref,
    table_ref,
    *refs,
):
    before_ref, middle_ref, after_ref, beyond_ref, ahead_ref = refs[:5]
    scan_ref, weight_ref, grad_ref, mask_ref, out_ref = refs[5:10]
    wide_ref, near_ref, far_ref, high_ref, low_ref = refs[10:]
    step = pl.program_id(0)
    tile_y = mask_ref.shape[1]
    wide = depth * tile_y

    @pl.when(step == 0)
    def _():
        gx = lax.axis_index("gx")
        gy = lax.axis_index("gy")
        below, over = (gy > 0, gy < sizes[1] - 1)
        begin = 0
        for band, inside in (
            (before_ref, gx > 0),
            (middle_ref, gx >= 0),
            (after_ref, gx < sizes[0] - 1),
        ):

            def convert(i, carry, begin=begin, band=band, inside=inside):
                base = pl.multiple_of((begin + i) * span_y, 8)
                for part, there, offset, count in (
                    (band[i], inside, 0, tile_y),
                    (beyond_ref[begin + i], jnp.logical_and(inside, over), tile_y, 8),
                    (ahead_ref[begin + i], jnp.logical_and(inside, below), tile_y + 8, 8),
                ):
                    value = jnp.where(there, part.astype(jnp.float32), 0.0)
                    wide_ref[pl.ds(base + offset, count), :] = value
                return carry

            lax.fori_loop(0, band.shape[0], convert, 0)
            begin += band.shape[0]

    def fetch(block, carry):
        for inner in range(4):
            y = block * 4 + inner
            for layer in range(depth):
                row = source_ref[(step * tile_y + y) * depth + layer]
                lanes = pl.ds(layer * 512, 512)
                near_ref[pl.ds(y, 1), lanes] = wide_ref[pl.ds(row, 1), lanes]
                far_ref[pl.ds(y, 1), lanes] = wide_ref[pl.ds(row + span_y, 1), lanes]
        return carry

    lax.fori_loop(0, tile_y // 4, fetch, 0)
    for layer in range(depth):
        for chunk in range(4):
            source = pl.ds(layer * 512 + chunk * 128, 128)
            lanes = pl.ds(chunk * 128, 128)
            weight = weight_ref[0, :, source].astype(jnp.float32)
            warped = weight * near_ref[:, source] + (1.0 - weight) * far_ref[:, source]
            image = scan_ref[0, :, source].astype(jnp.float32) - warped
            image = image.astype(jnp.bfloat16).astype(jnp.float32)
            image = image * mask_ref[0, :, source].astype(jnp.float32)
            for c in range(3):
                rows = pl.ds(c * wide + layer * tile_y, tile_y)
                value = image * grad_ref[c, 0, :, source].astype(jnp.float32)
                put_split(value, high_ref, low_ref, rows, lanes)
    table = table_ref[...]
    for c in range(3):
        rows = pl.ds(c * wide, wide)
        total = contract(table, high_ref[rows, :]) + contract(table, low_ref[rows, :])
        value = total[0:8] + total[8:16] + total[16:24]
        out_ref[c, :, pl.ds(step, 1), :] = value[:, None, :]


def solve_kernel(
    sizes,
    tile_y,
    hess_ref,
    load_ref,
    inc_ref,
    res_ref,
    field_ref,
    image_ref,
    out_x,
    out_y,
    out_c,
    in_x,
    in_y,
    in_c,
    own_x,
    got_x,
    own_y,
    got_y,
    send_sems,
    recv_sems,
    send_x,
    recv_x,
    send_y,
    recv_y,
):
    n_gx, n_gy = sizes
    tile_x, width = (hess_ref.shape[2], hess_ref.shape[3])
    gx = lax.axis_index("gx")
    gy = lax.axis_index("gy")
    in_x[...] = jnp.zeros_like(in_x)
    in_y[...] = jnp.zeros_like(in_y)
    in_c[...] = jnp.zeros_like(in_c)

    barrier = pltpu.get_barrier_semaphore()
    for k in range(1, n_gx):
        pl.semaphore_signal(barrier, inc=1, device_id=((gx + k) % n_gx, gy), device_id_type=MESH)
    for k in range(1, n_gy):
        pl.semaphore_signal(barrier, inc=1, device_id=(gx, (gy + k) % n_gy), device_id_type=MESH)
    low = jnp.logical_and(gx > 0, gy > 0)
    high = jnp.logical_and(gx < n_gx - 1, gy < n_gy - 1)

    @pl.when(low)
    def _():
        pl.semaphore_signal(barrier, inc=1, device_id=(gx - 1, gy - 1), device_id_type=MESH)

    @pl.when(high)
    def _():
        pl.semaphore_signal(barrier, inc=1, device_id=(gx + 1, gy + 1), device_id_type=MESH)

    corners = jnp.where(low, 1, 0) + jnp.where(high, 1, 0)
    pl.semaphore_wait(barrier, n_gx - 1 + n_gy - 1 + corners)

    lane = lax.broadcasted_iota(jnp.int32, (1, tile_x, width), 2)
    row = lax.broadcasted_iota(jnp.int32, (1, tile_x, width), 1)
    in_tile = lane % tile_y
    first_y = in_tile == 0
    last_y = in_tile == tile_y - 1
    first_x = row == 0
    last_x = row == tile_x - 1
    topmost = lane >= width - tile_y
    above = lane >= tile_y

    def copies(phase, dx, dy):
        def make(k, src, dst, target):
            return pltpu.make_async_remote_copy(
                src_ref=src.at[phase],
                dst_ref=dst.at[phase],
                send_sem=send_sems.at[phase, k],
                recv_sem=recv_sems.at[phase, k],
                device_id=target,
                device_id_type=MESH,
            )

        up = dx > 0
        send_gx, recv_gx = (gx < n_gx - 1, gx > 0) if up else (gx > 0, gx < n_gx - 1)
        send_gy, recv_gy = (gy < n_gy - 1, gy > 0) if up else (gy > 0, gy < n_gy - 1)
        return [
            (make(0, out_x, in_x, (gx + dx, gy)), send_gx, recv_gx),
            (make(1, out_y, in_y, (gx, gy + dy)), send_gy, recv_gy),
            (
                make(2, out_c, in_c, (gx + dx, gy + dy)),
                jnp.logical_and(send_gx, send_gy),
                jnp.logical_and(recv_gx, recv_gy),
            ),
        ]

    def start(phase, step):
        for copy, sends, _ in copies(phase, step, step):
            pl.when(sends)(copy.start)

    def arrive(phase, step):
        for copy, _, receives in copies(phase, step, step):
            pl.when(receives)(copy.wait_recv)

    def finish(phase, step):
        for copy, sends, _ in copies(phase, step, step):
            pl.when(sends)(copy.wait_send)

    def roll(value, shift, axis):
        return pltpu.roll(value, shift % value.shape[axis], axis)

    def shift_x(value):
        return jnp.where(first_x, 0.0, roll(value, 1, 1))

    def collect(phase, meanwhile):
        folded = {}
        for i in range(2):
            for j in range(2):
                under = image_ref[pl.ds((4 * i + 2 * j) * 3, 3)]
                over = image_ref[pl.ds((4 * i + 2 * j + 1) * 3, 3)]
                main = under + jnp.where(above, roll(over, tile_y, 2), 0.0)
                top = jnp.where(topmost, over, 0.0)
                folded[i, j] = jnp.concatenate([main, top], axis=0)
        kept, passed = ([], [])
        for i in range(2):
            kept.append(folded[i, 0] + jnp.where(first_y, 0.0, roll(folded[i, 1], 1, 2)))
            passed.append(jnp.where(first_y, roll(folded[i, 1], 1 - tile_y, 2), 0.0))
        out_x[phase] = kept[1][:, tile_x - 8 :, :]
        out_y[phase] = passed[0] + shift_x(passed[1])
        out_c[phase] = passed[1][:, tile_x - 8 :, :]
        start(phase, 1)
        total = kept[0] + shift_x(kept[1])
        meanwhile()
        arrive(phase, 1)
        edge = in_x[phase][:, 7:8, :] + in_c[phase][:, 7:8, :]
        return total + in_y[phase] + jnp.where(first_x, edge, 0.0)

    def spread(phase, field, meanwhile):
        turned = roll(field, tile_y - 1, 2)
        out_x[phase] = field[:, 0:8, :]
        out_y[phase] = turned
        out_c[phase] = turned[:, 0:8, :]
        start(phase, -1)
        meanwhile()
        next_x = roll(field, -1, 1)
        next_y = roll(field, -1, 2)

        def place(i, j, value):
            main, top = (value[0:3], value[3:6])
            field_ref[pl.ds((4 * i + 2 * j) * 3, 3)] = main
            field_ref[pl.ds((4 * i + 2 * j + 1) * 3, 3)] = jnp.where(
                topmost, top, roll(main, -tile_y, 2)
            )

        place(0, 0, field)
        arrive(phase, -1)
        side = in_x[phase]
        next_x = jnp.where(last_x, side[:, 0:1, :], next_x)
        next_y = jnp.where(last_y, in_y[phase], next_y)
        corner = jnp.where(last_y[:, 0:8], in_c[phase], roll(side, -1, 2))
        both = jnp.where(last_x, corner[:, 0:1, :], roll(next_y, -1, 1))
        place(1, 0, next_x)
        place(0, 1, next_y)
        place(1, 1, both)

    def apply():
        for n, (i, j, l) in enumerate(NODES):
            for c in range(3):
                total = None
                for m, (p, q, r) in enumerate(NODES):
                    kind = (i + p) * 9 + (j + q) * 3 + l + r
                    for d in range(3):
                        term = hess_ref[PAIR_OF[c, d], kind] * field_ref[3 * m + d]
                        total = term if total is None else total + term
                image_ref[3 * n + c] = total

    def exchange(own, got, sends, receives, slot, index, count, target):
        return [
            pltpu.make_async_remote_copy(
                src_ref=own.at[slot],
                dst_ref=got.at[slot, k - 1],
                send_sem=sends.at[slot, k - 1],
                recv_sem=receives.at[slot, k - 1],
                device_id=target((index + k) % count),
                device_id_type=MESH,
            )
            for k in range(1, count)
        ]

    def along_x(slot):
        return exchange(own_x, got_x, send_x, recv_x, slot, gx, n_gx, lambda t: (t, gy))

    def along_y(slot):
        return exchange(own_y, got_y, send_y, recv_y, slot, gy, n_gy, lambda t: (gx, t))

    def total_of(copies, own, got, slot, index, count):
        for copy in copies:
            copy.wait_recv()
        others = [got[slot, k - 1] for k in range(1, count)]
        return in_order(index, count, own[slot], others)

    def in_order(index, count, mine, others):
        total = jnp.zeros_like(mine)
        for source in range(count):
            value = jnp.where(index == source, mine, 0.0)
            for k in range(1, count):
                value = jnp.where((index - k + count) % count == source, others[k - 1], value)
            total = total + value
        return total

    def open_products(slot, vector, image):
        one = jnp.sum(jnp.sum(vector * vector, axis=0), axis=0, keepdims=True)
        two = jnp.sum(jnp.sum(vector * image, axis=0), axis=0, keepdims=True)
        line = lax.broadcasted_iota(jnp.int32, (8, width), 0)
        own_x[slot] = jnp.where(line == 0, one, jnp.where(line == 1, two, 0.0))
        for copy in along_x(slot):
            copy.start()

    def pass_products(slot):
        own_y[slot] = total_of(along_x(slot), own_x, got_x, slot, gx, n_gx)
        for copy in along_y(slot):
            copy.start()

    def close_products(slot):
        total = total_of(along_y(slot), own_y, got_y, slot, gy, n_gy)
        return (
            jnp.sum(total[0:1], axis=1, keepdims=True)[None],
            jnp.sum(total[1:2], axis=1, keepdims=True)[None],
        )

    def nothing():
        return None

    def operate(phase, field, during_spread=nothing, during_collect=nothing):
        spread(phase, field, during_spread)
        apply()
        return collect(phase + 1, during_collect) + tikhonov * field

    for c in range(3):
        for n in range(8):
            image_ref[3 * n + c] = load_ref[c, n]
    rhs = collect(0, nothing)
    increment = jnp.zeros_like(rhs)
    residual = rhs
    image = operate(1, residual)
    for sweep in range(ITERS):
        if sweep + 1 < ITERS:
            second = operate(
                2 * sweep + 3,
                image,
                lambda: open_products(sweep, residual, image),
                lambda: pass_products(sweep),
            )
        else:
            open_products(sweep, residual, image)
            pass_products(sweep)
        norm_next, product = close_products(sweep)
        if sweep == 0:
            step_size = norm_next / product
            direction, along = (residual, image)
        else:
            factor = norm_next / norm_now
            step_size = norm_next / (product - factor * norm_next / step_size)
            direction = residual + factor * direction
            along = image + factor * along
        norm_now = norm_next
        increment = increment + step_size * direction
        residual = residual - step_size * along
        if sweep + 1 < ITERS:
            deep = second if sweep == 0 else second + factor * deep
            image = image - step_size * deep
    inc_ref[...] = increment
    res_ref[...] = residual
    finish(0, 1)
    for sweep in range(ITERS):
        finish(2 * sweep + 1, -1)
        finish(2 * sweep + 2, 1)
        for copy in along_x(sweep) + along_y(sweep):
            copy.wait_send()


def per_device(
    reference_scan, ref_gradient, deformed_scan, interp_weights, sample_mask, block_list, offsets
):
    tile_x, tile_y, column = reference_scan.shape
    depth = column // 512
    width = depth * tile_y
    square_table, shape_table = tables()

    n_gx, n_gy = (lax.axis_size("gx"), lax.axis_size("gy"))
    span_x, span_y = (tile_x + 2 * BOUND + 1, tile_y + 16)
    pos_x = jnp.arange(tile_x)[:, None, None]
    pos_y = jnp.arange(tile_y)[None, :, None]
    source = (pos_x + offsets[0] + BOUND) * span_y + (pos_y + offsets[1] + span_y) % span_y

    voxels = pl.BlockSpec((1, tile_y, column), lambda x: (x, 0, 0))
    gradients = pl.BlockSpec((3, 1, tile_y, column), lambda x: (0, x, 0, 0))
    vmem = pl.BlockSpec(memory_space=pltpu.VMEM)
    size = tile_x * tile_y * column
    anywhere = pl.BlockSpec(memory_space=pl.ANY)
    hessian, before, after, beyond, ahead = pl.pallas_call(
        functools.partial(hessian_kernel, depth, (n_gx, n_gy)),
        grid=(tile_x,),
        out_shape=[jax.ShapeDtypeStruct((6, 32, tile_x, width), jnp.float32)]
        + [
            jax.ShapeDtypeStruct(extent + (column,), jnp.bfloat16)
            for extent in (
                (BOUND, tile_y),
                (BOUND + 1, tile_y),
                (tile_x + 2 * BOUND + 1, 8),
                (tile_x + 2 * BOUND + 1, 8),
            )
        ],
        in_specs=[pl.BlockSpec((96, 512), lambda x: (0, 0)), gradients, voxels, anywhere],
        out_specs=[pl.BlockSpec((6, 32, tile_x, width), lambda x: (0, 0, 0, 0))] + [anywhere] * 4,
        scratch_shapes=[pltpu.VMEM((6 * width, 512), jnp.bfloat16)] * 2
        + [pltpu.SemaphoreType.DMA((8,))] * 2,
        compiler_params=pltpu.CompilerParams(collective_id=1, has_side_effects=True),
        cost_estimate=pl.CostEstimate(
            flops=size * 6 * 2 * 256, bytes_accessed=size * 10, transcendentals=0
        ),
        name="hessian",
    )(square_table, ref_gradient, sample_mask, deformed_scan)
    pieces = [before, deformed_scan, after, beyond, ahead]
    load = pl.pallas_call(
        functools.partial(load_kernel, depth, span_y, (n_gx, n_gy)),
        grid=(tile_x,),
        out_shape=jax.ShapeDtypeStruct((3, 8, tile_x, width), jnp.float32),
        in_specs=[
            pl.BlockSpec(memory_space=pltpu.SMEM),
            pl.BlockSpec((32, 512), lambda x: (0, 0)),
        ]
        + [pl.BlockSpec(piece.shape, lambda x: (0, 0, 0)) for piece in pieces]
        + [
            voxels,
            voxels,
            gradients,
            voxels,
        ],
        out_specs=pl.BlockSpec((3, 8, tile_x, width), lambda x: (0, 0, 0, 0)),
        scratch_shapes=[
            pltpu.VMEM((span_x * span_y, column), jnp.float32),
            pltpu.VMEM((tile_y, column), jnp.float32),
            pltpu.VMEM((tile_y, column), jnp.float32),
            pltpu.VMEM((3 * width, 512), jnp.bfloat16),
            pltpu.VMEM((3 * width, 512), jnp.bfloat16),
        ],
        name="load",
    )(
        source.reshape(-1),
        shape_table,
        *pieces,
        reference_scan,
        interp_weights,
        ref_gradient,
        sample_mask,
    )
    n_gx, n_gy = (lax.axis_size("gx"), lax.axis_size("gy"))
    phases = 2 * ITERS + 1
    part = jax.ShapeDtypeStruct((6, tile_x, width), jnp.float32)
    dma = pltpu.SemaphoreType.DMA
    increment, residual = pl.pallas_call(
        functools.partial(solve_kernel, (n_gx, n_gy), tile_y),
        out_shape=(part, part),
        in_specs=[vmem, vmem],
        out_specs=(vmem, vmem),
        scratch_shapes=[
            pltpu.VMEM((24, tile_x, width), jnp.float32),
            pltpu.VMEM((24, tile_x, width), jnp.float32),
        ]
        + [
            pltpu.VMEM((phases, 6, rows, width), jnp.float32)
            for rows in (8, tile_x, 8, 8, tile_x, 8)
        ]
        + [
            pltpu.VMEM((ITERS, 8, width), jnp.float32),
            pltpu.VMEM((ITERS, n_gx - 1, 8, width), jnp.float32),
            pltpu.VMEM((ITERS, 8, width), jnp.float32),
            pltpu.VMEM((ITERS, n_gy - 1, 8, width), jnp.float32),
            dma((phases, 3)),
            dma((phases, 3)),
            dma((ITERS, n_gx - 1)),
            dma((ITERS, n_gx - 1)),
            dma((ITERS, n_gy - 1)),
            dma((ITERS, n_gy - 1)),
        ],
        compiler_params=pltpu.CompilerParams(collective_id=0, has_side_effects=True),
        name="solve",
    )(hessian, load)

    def nodal(value):
        main = jnp.transpose(value[:3].reshape(3, tile_x, depth, tile_y), (0, 1, 3, 2))
        return jnp.concatenate([main, value[3:, :, width - tile_y :, None]], axis=3)

    return (nodal(increment), nodal(residual))


def solution(mesh):
    return jax.shard_map(
        per_device,
        mesh=mesh,
        in_specs=(
            P("gx", "gy", None),
            P(None, "gx", "gy", None),
            P("gx", "gy", None),
            P("gx", "gy", None),
            P("gx", "gy", None),
            P("gx", "gy"),
            P(None, "gx", "gy", None),
        ),
        out_specs=(P(None, "gx", "gy", None), P(None, "gx", "gy", None)),
        check_vma=False,
    )
```
